512 devices in a mesh: sec: 16 (over z_lo, y), tile: 32 (over x, z_hi, core).
Axes of the slice: x: 4, y: 4, z: 16 (z_hi: 4, z_lo: 4; z = z_hi * 4 + z_lo), core: 2. Of those that a mesh axis runs over, the one named last changes fastest.
Arguments:
- snapshots: bfloat16 [5, 256, 3072, 256], P(None, 'sec', 'tile'), may hold values from -6 to 6
- eig_columns: bfloat16 [256, 256], P(None, 'tile'), may hold values from -0.375 to 0.375
- mean_u: float32 [256, 3072], P('sec', 'tile'), may hold values from 0.2 to 1
- mean_v: float32 [256, 3072], P('sec', 'tile'), may hold values from -0.5 to 0.5
- mean_rho: float32 [256, 3072], P('sec', 'tile'), may hold values from 0.5 to 2
- mean_shear: float32 [256, 3072], P('sec', 'tile'), may hold values from 0.2 to 2
- sound: float32 [256, 3072], P('sec', 'tile'), may hold values from 0.5 to 4
Outputs:
- rayleigh: float32 [16, 256, 256], P('sec', 'tile')
The draws below stay inside these ranges and needn't reach their ends.
All inputs are finite; a program needn't handle non-finite values.
Results may differ from the reference program's by a relative error of at most 0.0044.
Values may be sent and summed in bfloat16 or wider, within the bound.
No kernel may reach another device: no remote copies, remote signals or barrier semaphores. Data moves between devices by JAX's collectives and lax.ppermute only.
A program may use at most 64 MiB of HBM per device.

```python
import math
import jax
import jax.numpy as jnp
from jax import lax

M = 256
S = 256
CX = 16
NX = 256
NY = 3072
N_SEC = 16


def steps_of(stream_key, extent, cuts, low, top_value):
    loudness = 1.0
    for axis_at, shards_of in cuts:
        draws = jax.random.uniform(jax.random.fold_in(jax.random.fold_in(stream_key, 6), axis_at), (shards_of,), jnp.float32, low / len(cuts), top_value / len(cuts))
        loudness = loudness * jnp.repeat(jnp.exp(draws), extent[axis_at] // shards_of).reshape((-1,) + (1,) * (len(extent) - 1 - axis_at))
    return loudness


def centred(rng, shape, spread, limit, split=(), held_as=jnp.bfloat16):
    array = jax.random.normal(rng, shape, jnp.float32) * spread
    if len(split) > 0:
        array = steps_of(rng, shape, split, -0.22, 0.18) * array
    return jnp.clip(array, min=-limit, max=limit).astype(held_as)


def setup_inputs(seed: int = 0) -> dict:
    arg_keys = jax.random.split(jax.random.key(seed), 8)
    return {
        "snapshots": centred(arg_keys[0], (5, NX, NY, S), 1.0, 6.0, ((1, 16), (2, 32))),
        "eig_columns": centred(arg_keys[1], (S, M), S ** -0.5, 0.375, ((1, 32),)),
        "mean_u": jnp.clip(0.2 + 0.8 * jax.random.uniform(arg_keys[2], (NX, NY), jnp.float32) ** steps_of(arg_keys[2], (NX, NY), ((0, 16), (1, 32)), -0.2, 0.2), 0.2, 1.0),
        "mean_v": jnp.clip(jax.random.uniform(arg_keys[3], (NX, NY), jnp.float32, -0.5, 0.5) * steps_of(arg_keys[3], (NX, NY), ((0, 16), (1, 32)), -0.4, 0.0), -0.5, 0.5),
        "mean_rho": jnp.clip(jnp.exp(math.log(2.0) - 1.3862944 * jax.random.uniform(arg_keys[4], (NX, NY), jnp.float32) ** steps_of(arg_keys[4], (NX, NY), ((0, 16), (1, 32)), -0.2, 0.2)), 0.5, 2.0),
        "mean_shear": jnp.clip(jnp.exp(math.log(2.0) - 2.3025851 * jax.random.uniform(arg_keys[5], (NX, NY), jnp.float32) ** steps_of(arg_keys[5], (NX, NY), ((0, 16), (1, 32)), -0.2, 0.2)), 0.2, 2.0),
        "sound": jnp.clip(jnp.exp(math.log(4.0) - 2.0794415 * jax.random.uniform(arg_keys[6], (NX, NY), jnp.float32) ** steps_of(arg_keys[6], (NX, NY), ((0, 16), (1, 32)), -0.2, 0.2)), 0.5, 4.0),
    }


viscosity = 0.002


def field_at(padded, k, off_x, off_y):
    end_x = padded.shape[1] - 1 + off_x
    end_y = padded.shape[2] - 1 + off_y
    return padded[k, 1 + off_x:end_x, 1 + off_y:end_y, :].astype(jnp.float32)


def gradient(padded, k):
    along_x = (field_at(padded, k, 1, 0) - field_at(padded, k, -1, 0)) * 0.5
    along_y = (field_at(padded, k, 0, 1) - field_at(padded, k, 0, -1)) * 0.5
    return along_x, along_y


def laplace(padded, k):
    total = field_at(padded, k, 1, 0) + field_at(padded, k, -1, 0)
    total = total + field_at(padded, k, 0, 1) + field_at(padded, k, 0, -1)
    return total - 4.0 * field_at(padded, k, 0, 0)


def stencil(padded, mean_u, mean_v, mean_rho, mean_shear, sound):
    flow_x = mean_u[:, :, None]
    flow_y = mean_v[:, :, None]
    density = mean_rho[:, :, None]
    inverse = 1.0 / density
    shear = mean_shear[:, :, None]
    stiff = sound[:, :, None]
    rho_x, rho_y = gradient(padded, 0)
    u_x, u_y = gradient(padded, 1)
    v_x, v_y = gradient(padded, 2)
    w_x, w_y = gradient(padded, 3)
    p_x, p_y = gradient(padded, 4)
    diverge = u_x + v_y
    image_rho = -(flow_x * rho_x + flow_y * rho_y) - density * diverge
    image_u = -(flow_x * u_x + flow_y * u_y) - shear * field_at(padded, 2, 0, 0) - inverse * p_x + viscosity * laplace(padded, 1)
    image_v = -(flow_x * v_x + flow_y * v_y) - inverse * p_y + viscosity * laplace(padded, 2)
    image_w = -(flow_x * w_x + flow_y * w_y) + viscosity * laplace(padded, 3)
    image_p = -(flow_x * p_x + flow_y * p_y) - stiff * diverge
    return jnp.stack([image_rho, image_u, image_v, image_w, image_p]).astype(jnp.bfloat16)


def reference(snapshots, eig_columns, mean_u, mean_v, mean_rho, mean_shear, sound):
    scale = float(5 * NX * NY) ** -0.5
    padded_all = jnp.pad(snapshots, ((0, 0), (1, 1), (0, 0), (0, 0)))
    eig_wide = eig_columns.astype(jnp.float32)
    zero = jnp.int32(0)

    def section(index):
        start = (index * CX).astype(jnp.int32)
        slab = lax.dynamic_slice(padded_all, (zero, start, zero, zero), (5, CX + 2, NY, S))
        modes = jnp.einsum('fxys,sk->fxyk', slab.astype(jnp.float32), eig_wide).astype(jnp.bfloat16)
        padded = jnp.pad(modes, ((0, 0), (0, 0), (1, 1), (0, 0)))
        cut_u = lax.dynamic_slice_in_dim(mean_u, start, CX, 0)
        cut_v = lax.dynamic_slice_in_dim(mean_v, start, CX, 0)
        cut_rho = lax.dynamic_slice_in_dim(mean_rho, start, CX, 0)
        cut_shear = lax.dynamic_slice_in_dim(mean_shear, start, CX, 0)
        cut_sound = lax.dynamic_slice_in_dim(sound, start, CX, 0)
        image = stencil(padded, cut_u, cut_v, cut_rho, cut_shear, cut_sound)
        interior = modes[:, 1:-1]
        return jnp.einsum('fxyk,fxyl->kl', interior.astype(jnp.float32), image.astype(jnp.float32)) * scale

    terms = lax.map(section, jnp.arange(N_SEC, dtype=jnp.int32))
    return jnp.cumsum(terms, axis=0)
```

```python
import jax
import jax.numpy as jnp
from jax import lax
from jax.experimental import pallas as pl
from jax.experimental.pallas import tpu as pltpu
from jax.sharding import PartitionSpec as P

viscosity = 0.002
pad = 8
strip = 16


def interior_kernel(x_hbm, mu, mv, mr, ms, mc, g_ref, ct_ref, xb, qf, raw, image, sems):
    fields, nx, ny, modes = x_hbm.shape

    def copy(i):
        return pltpu.make_async_copy(x_hbm.at[:, i], xb.at[i], sems.at[i])

    for i in range(nx):
        copy(i).start()

    raw[...] = jnp.zeros_like(raw)
    for j, value in enumerate(
        (mu[...] * -0.5, mv[...] * -0.5, mr[...] * -0.5, -ms[...], -0.5 / mr[...], mc[...] * -0.5)
    ):
        raw[j * nx : (j + 1) * nx, 0:ny] = value
    ct_ref[...] = raw[...].T
    qf[0] = jnp.zeros(qf.shape[1:], jnp.float32)
    qf[nx + 1] = jnp.zeros(qf.shape[1:], jnp.float32)
    g_ref[...] = jnp.zeros_like(g_ref)

    def widen(i):
        copy(i).wait()
        edge = jnp.zeros((pad, modes), jnp.float32)
        for f in range(fields):
            qf[i + 1, f, 0:pad] = edge
            qf[i + 1, f, pad + ny : 2 * pad + ny] = edge
            for y in range(0, ny, strip):
                qf[i + 1, f, pad + y : pad + y + strip] = xb[i, f, y : y + strip].astype(jnp.float32)

    def apply(i):
        turned = pltpu.roll(ct_ref[...], 128 - i, 1)
        for y in range(0, ny, strip):
            column = turned[y : y + strip]
            half_u, half_v, half_rho, shear, half_inverse, half_sound = (
                jnp.broadcast_to(column[:, j * nx : j * nx + 1], (strip, modes)) for j in range(6)
            )
            east_c, west_c = viscosity + half_u, viscosity - half_u
            north_c, south_c = viscosity + half_v, viscosity - half_v
            top = pad + y

            def east(f):
                return qf[i + 2, f, top : top + strip]

            def west(f):
                return qf[i, f, top : top + strip]

            def north(f):
                return qf[i + 1, f, top + 1 : top + 1 + strip]

            def south(f):
                return qf[i + 1, f, top - 1 : top - 1 + strip]

            def here(f):
                return qf[i + 1, f, top : top + strip]

            def flow(f):
                return half_u * (east(f) - west(f)) + half_v * (north(f) - south(f))

            def spread(f):
                return (
                    east_c * east(f) + west_c * west(f) + north_c * north(f) + south_c * south(f)
                ) - (4.0 * viscosity) * here(f)

            diverge = (east(1) - west(1)) + (north(2) - south(2))
            images = (
                flow(0) + half_rho * diverge,
                spread(1) + shear * here(2) + half_inverse * (east(4) - west(4)),
                spread(2) + half_inverse * (north(4) - south(4)),
                spread(3),
                flow(4) + half_sound * diverge,
            )
            for f in range(fields):
                high = images[f].astype(jnp.bfloat16)
                low = (images[f] - high.astype(jnp.float32)).astype(jnp.bfloat16)
                image[f * ny + y : f * ny + y + strip, 0:modes] = high
                image[f * ny + y : f * ny + y + strip, modes : 2 * modes] = low
        g_ref[...] += lax.dot_general(
            xb[i].reshape(fields * ny, modes),
            image[...],
            (((0,), (0,)), ((), ())),
            preferred_element_type=jnp.float32,
        )

    widen(0)

    def step(i, carry):
        @pl.when(i + 1 < nx)
        def _():
            widen(i + 1)

        apply(i)
        return carry

    lax.fori_loop(0, nx, step, 0)


def interior(snapshots, *means):
    fields, nx, ny, modes = snapshots.shape
    return pl.pallas_call(
        interior_kernel,
        out_shape=(
            jax.ShapeDtypeStruct((modes, 2 * modes), jnp.float32),
            jax.ShapeDtypeStruct((128, 128), jnp.float32),
        ),
        in_specs=[pl.BlockSpec(memory_space=pltpu.HBM)] + [pl.BlockSpec(memory_space=pltpu.VMEM)] * 5,
        out_specs=(pl.BlockSpec(memory_space=pltpu.VMEM),) * 2,
        scratch_shapes=[
            pltpu.VMEM((nx, fields, ny, modes), jnp.bfloat16),
            pltpu.VMEM((nx + 2, fields, ny + 2 * pad, modes), jnp.float32),
            pltpu.VMEM((128, 128), jnp.float32),
            pltpu.VMEM((fields * ny, 2 * modes), jnp.bfloat16),
            pltpu.SemaphoreType.DMA((nx,)),
        ],
        compiler_params=pltpu.CompilerParams(vmem_limit_bytes=20 << 20),
        cost_estimate=pl.CostEstimate(flops=20 * 10**9, transcendentals=0, bytes_accessed=10**7),
        name="interior",
    )(snapshots, *means)


def split(value):
    high = value.astype(jnp.bfloat16)
    rest = value - high.astype(jnp.float32)
    middle = rest.astype(jnp.bfloat16)
    return high, middle, (rest - middle.astype(jnp.float32)).astype(jnp.bfloat16)


def contract(left, right):
    return lax.dot_general(left, right, (((0,), (0,)), ((), ())), preferred_element_type=jnp.float32)


def finish_kernel(
    scale, g_ref, ct_ref, head_x, tail_x, from_west, from_east, tail_y, from_north,
    mv, mr, mc, vt_ref, out_ref
):
    modes = g_ref.shape[0]
    ny = head_x.shape[2]
    nx = tail_y.shape[1]
    total = g_ref[:, 0:modes] + g_ref[:, modes : 2 * modes]

    def side(own, other, column, along, cross, sign):
        half_c, half_rho, half_inverse, half_sound = (sign * c for c in column)
        spread_c = viscosity + half_c
        images = [
            half_c * other(0) + half_rho * other(along),
            spread_c * other(1),
            spread_c * other(2),
            spread_c * other(3),
            half_c * other(4) + half_sound * other(along),
        ]
        images[along] = images[along] + half_inverse * other(4)
        added = None
        for f in range(5):
            high, middle, _ = split(images[f])
            one = contract(own(f), high) + contract(own(f), middle)
            added = one if added is None else added + one
        return added

    def plane(ref):
        return lambda f: ref[f, 0].astype(jnp.float32)

    def column_x(i):
        return tuple(ct_ref[0:ny, j * nx + i : j * nx + i + 1] for j in (0, 2, 4, 5))

    total += side(lambda f: head_x[f, 0], plane(from_west), column_x(0), 1, 2, -1.0)
    total += side(lambda f: tail_x[f, 0], plane(from_east), column_x(nx - 1), 1, 2, 1.0)

    own_column = tuple(
        c for c in (mv[:, ny - 1 : ny] * -0.5, mr[:, ny - 1 : ny] * -0.5, -0.5 / mr[:, ny - 1 : ny], mc[:, ny - 1 : ny] * -0.5)
    )
    packed = from_north[5].astype(jnp.float32)
    other_column = tuple(
        packed[:, 3 * j : 3 * j + 1] + packed[:, 3 * j + 1 : 3 * j + 2] + packed[:, 3 * j + 2 : 3 * j + 3]
        for j in range(4)
    )
    wide = lambda ref: (lambda f: ref[f].astype(jnp.float32))
    total += side(lambda f: tail_y[f], wide(from_north), own_column, 2, 1, 1.0)
    total += side(lambda f: from_north[f], wide(tail_y), other_column, 2, 1, -1.0)

    vt = vt_ref[...]
    right = None
    for part in split(total):
        one = lax.dot_general(part, vt, (((1,), (1,)), ((), ())), preferred_element_type=jnp.float32)
        right = one if right is None else right + one
    both = None
    for part in split(right):
        one = jnp.dot(vt, part, preferred_element_type=jnp.float32)
        both = one if both is None else both + one
    out_ref[...] = (both * scale).astype(out_ref.dtype)


def finish(scale, *operands):
    import functools

    modes = operands[-1].shape[0]
    return pl.pallas_call(
        functools.partial(finish_kernel, scale),
        out_shape=jax.ShapeDtypeStruct((modes, modes), jnp.float32),
        in_specs=[pl.BlockSpec(memory_space=pltpu.VMEM)] * len(operands),
        out_specs=pl.BlockSpec(memory_space=pltpu.VMEM),
        compiler_params=pltpu.CompilerParams(vmem_limit_bytes=12 << 20),
        name="finish",
    )(*operands)


def pieces(value):
    high = lax.reduce_precision(value, 8, 7)
    rest = value - high
    middle = lax.reduce_precision(rest, 8, 7)
    return [high, middle, rest - middle]


def body(snapshots, eig_columns, mean_u, mean_v, mean_rho, mean_shear, sound):
    sections = lax.axis_size("sec")
    tiles_n = lax.axis_size("tile")
    fields, nx, ny, modes = snapshots.shape
    rows = modes // tiles_n
    scale = float(fields * nx * ny * sections * tiles_n) ** (-0.5)

    first = (mean_v[:, 0], mean_rho[:, 0], sound[:, 0])
    sent = [first[0] * -0.5, first[1] * -0.5, -0.5 / first[1], first[2] * -0.5]
    packed = jnp.stack([p for value in sent for p in pieces(value)], axis=-1)
    packed = jnp.pad(packed, ((0, 0), (0, modes - packed.shape[1])))
    head_y = jnp.concatenate([snapshots[:, :, 0], packed[None].astype(jnp.bfloat16)])
    tail_y = snapshots[:, :, ny - 1]
    from_north = lax.ppermute(head_y, "tile", [(i + 1, i) for i in range(tiles_n - 1)])
    own = jnp.broadcast_to(eig_columns.T[None], (tiles_n, rows, modes))
    vt = lax.all_to_all(own, "tile", 0, 0, tiled=True).reshape(modes, modes)
    head_x = snapshots[:, :1]
    tail_x = snapshots[:, nx - 1 :]
    from_west = lax.ppermute(tail_x, "sec", [(i, i + 1) for i in range(sections - 1)])
    from_east = lax.ppermute(head_x, "sec", [(i + 1, i) for i in range(sections - 1)])

    gram, columns = interior(snapshots, mean_u, mean_v, mean_rho, mean_shear, sound)
    local = finish(
        scale, gram, columns, head_x, tail_x, from_west, from_east, tail_y, from_north,
        mean_v, mean_rho, sound, vt
    )
    shares = lax.all_to_all(local.reshape(tiles_n, rows, modes), "tile", 0, 0, tiled=True)
    term = shares.sum(0)
    terms = lax.all_to_all(
        jnp.broadcast_to(term[None], (sections, rows, modes)), "sec", 0, 0, tiled=True
    )
    upstream = jnp.arange(sections) <= lax.axis_index("sec")
    return jnp.where(upstream[:, None, None], terms, 0.0).sum(0)[None]


def solution(mesh):
    in_specs = (
        P(None, "sec", "tile", None),
        P(None, "tile"),
        P("sec", "tile"),
        P("sec", "tile"),
        P("sec", "tile"),
        P("sec", "tile"),
        P("sec", "tile"),
    )
    out_specs = P("sec", "tile", None)
    return jax.shard_map(body, mesh=mesh, in_specs=in_specs, out_specs=out_specs, check_vma=False)
```

```python
import functools

import jax
import jax.numpy as jnp
from jax import lax
from jax.experimental import pallas as pl
from jax.experimental.pallas import tpu as pltpu
from jax.sharding import PartitionSpec as P

viscosity = 0.002
pad = 8
strip = 16


def interior_kernel(x_hbm, mu_hbm, mv_hbm, mr_hbm, ms_hbm, mc_hbm, g_ref, raw, ct_ref, xb, qf, means, image, sems):
    fields, nx, ny, modes = x_hbm.shape

    def copy(i):
        return pltpu.make_async_copy(x_hbm.at[:, i], xb.at[i], sems.at[i])

    coefficients = [
        pltpu.make_async_copy(ref, means.at[j], sems.at[nx + j])
        for j, ref in enumerate((mu_hbm, mv_hbm, mr_hbm, ms_hbm, mc_hbm))
    ]
    for one in coefficients:
        one.start()
    for i in range(nx):
        copy(i).start()

    raw[...] = jnp.zeros_like(raw)
    for one in coefficients:
        one.wait()
    u, v, rho, shear_u, stiff = (means[j] for j in range(5))
    for j, value in enumerate((u * -0.5, v * -0.5, rho * -0.5, -shear_u, -0.5 / rho, stiff * -0.5)):
        raw[j * nx : (j + 1) * nx, 0:ny] = value
    ct_ref[...] = raw[...].T
    qf[0] = jnp.zeros(qf.shape[1:], jnp.float32)
    qf[nx + 1] = jnp.zeros(qf.shape[1:], jnp.float32)
    g_ref[...] = jnp.zeros_like(g_ref)

    def widen(i):
        copy(i).wait()
        edge = jnp.zeros((pad, modes), jnp.float32)
        for f in range(fields):
            qf[i + 1, f, 0:pad] = edge
            qf[i + 1, f, pad + ny : 2 * pad + ny] = edge
            for y in range(0, ny, strip):
                qf[i + 1, f, pad + y : pad + y + strip] = xb[i, f, y : y + strip].astype(jnp.float32)

    def apply(i):
        turned = pltpu.roll(ct_ref[...], 128 - i, 1)
        for y in range(0, ny, strip):
            column = turned[y : y + strip]
            half_u, half_v, half_rho, shear, half_inverse, half_sound = (
                jnp.broadcast_to(column[:, j * nx : j * nx + 1], (strip, modes)) for j in range(6)
            )
            east_c, west_c = viscosity + half_u, viscosity - half_u
            north_c, south_c = viscosity + half_v, viscosity - half_v
            top = pad + y

            def east(f):
                return qf[i + 2, f, top : top + strip]

            def west(f):
                return qf[i, f, top : top + strip]

            def north(f):
                return qf[i + 1, f, top + 1 : top + 1 + strip]

            def south(f):
                return qf[i + 1, f, top - 1 : top - 1 + strip]

            def here(f):
                return qf[i + 1, f, top : top + strip]

            def flow(f):
                return half_u * (east(f) - west(f)) + half_v * (north(f) - south(f))

            def spread(f):
                return (
                    east_c * east(f) + west_c * west(f) + north_c * north(f) + south_c * south(f)
                ) - (4.0 * viscosity) * here(f)

            diverge = (east(1) - west(1)) + (north(2) - south(2))
            images = (
                flow(0) + half_rho * diverge,
                spread(1) + shear * here(2) + half_inverse * (east(4) - west(4)),
                spread(2) + half_inverse * (north(4) - south(4)),
                spread(3),
                flow(4) + half_sound * diverge,
            )
            for f in range(fields):
                high = images[f].astype(jnp.bfloat16)
                low = (images[f] - high.astype(jnp.float32)).astype(jnp.bfloat16)
                image[f * ny + y : f * ny + y + strip, 0:modes] = high
                image[f * ny + y : f * ny + y + strip, modes : 2 * modes] = low
        g_ref[...] += lax.dot_general(
            xb[i].reshape(fields * ny, modes),
            image[...],
            (((0,), (0,)), ((), ())),
            preferred_element_type=jnp.float32,
        )

    widen(0)

    def step(i, carry):
        @pl.when(i + 1 < nx)
        def _():
            widen(i + 1)

        apply(i)
        return carry

    lax.fori_loop(0, nx, step, 0)


def interior(snapshots, *means):
    fields, nx, ny, modes = snapshots.shape
    return pl.pallas_call(
        interior_kernel,
        out_shape=(
            jax.ShapeDtypeStruct((modes, 2 * modes), jnp.float32),
            jax.ShapeDtypeStruct((128, 128), jnp.float32),
            jax.ShapeDtypeStruct((128, 128), jnp.float32),
        ),
        in_specs=[pl.BlockSpec(memory_space=pltpu.HBM)] * 6,
        out_specs=(pl.BlockSpec(memory_space=pltpu.VMEM),) * 3,
        scratch_shapes=[
            pltpu.VMEM((nx, fields, ny, modes), jnp.bfloat16),
            pltpu.VMEM((nx + 2, fields, ny + 2 * pad, modes), jnp.float32),
            pltpu.VMEM((5, nx, ny), jnp.float32),
            pltpu.VMEM((fields * ny, 2 * modes), jnp.bfloat16),
            pltpu.SemaphoreType.DMA((nx + 5,)),
        ],
        compiler_params=pltpu.CompilerParams(vmem_limit_bytes=20 << 20),
        cost_estimate=pl.CostEstimate(flops=20 * 10**9, transcendentals=0, bytes_accessed=10**7),
        name="interior",
    )(*(pltpu.with_memory_space_constraint(a, pltpu.HBM) for a in (snapshots, *means)))


def split(value):
    high = value.astype(jnp.bfloat16)
    rest = value - high.astype(jnp.float32)
    middle = rest.astype(jnp.bfloat16)
    return high, middle, (rest - middle.astype(jnp.float32)).astype(jnp.bfloat16)


def outline_kernel(x_hbm, eig_ref, mv_hbm, mr_hbm, mc_hbm, own_ref, head_y, tail_y, head_x, tail_x, low, high, means, sems):
    fields, nx, ny, modes = x_hbm.shape
    copies = [
        pltpu.make_async_copy(x_hbm.at[:, :, 0:strip], low, sems.at[0]),
        pltpu.make_async_copy(x_hbm.at[:, :, ny - strip : ny], high, sems.at[1]),
        pltpu.make_async_copy(x_hbm.at[:, 0], head_x, sems.at[2]),
        pltpu.make_async_copy(x_hbm.at[:, nx - 1], tail_x, sems.at[3]),
        pltpu.make_async_copy(mv_hbm, means.at[0], sems.at[4]),
        pltpu.make_async_copy(mr_hbm, means.at[1], sems.at[5]),
        pltpu.make_async_copy(mc_hbm, means.at[2], sems.at[6]),
    ]
    for copy in copies:
        copy.start()
    for t in range(own_ref.shape[0]):
        own_ref[t] = eig_ref[...]
    rows = lax.broadcasted_iota(jnp.int32, (nx, nx * strip), 0)
    cells = lax.broadcasted_iota(jnp.int32, (nx, nx * strip), 1)
    lanes = lax.broadcasted_iota(jnp.int32, (nx, modes), 1)
    for at, held, source, edge in ((0, low, head_y, 0), (1, high, tail_y, strip - 1)):
        chosen = jnp.where(cells == rows * strip + edge, 1.0, 0.0).astype(jnp.bfloat16)
        copies[at].wait()
        for f in range(fields):
            picked = jnp.dot(
                chosen, held[f].reshape(nx * strip, modes), preferred_element_type=jnp.float32
            )
            source[f] = picked.astype(jnp.bfloat16)
    for copy in copies[4:]:
        copy.wait()
    v, rho, stiff = (means[j, :, 0:1] for j in range(3))
    packed = jnp.zeros((nx, modes), jnp.float32)
    for j, value in enumerate((v * -0.5, rho * -0.5, -0.5 / rho, stiff * -0.5)):
        for p, part in enumerate(split(value)):
            packed = jnp.where(lanes == 3 * j + p, part.astype(jnp.float32), packed)
    head_y[fields] = packed.astype(jnp.bfloat16)
    copies[2].wait()
    copies[3].wait()


def outline(snapshots, eig_rows, tiles_n, mean_v, mean_rho, sound):
    fields, nx, ny, modes = snapshots.shape
    narrow = jnp.bfloat16
    in_hbm = [pltpu.with_memory_space_constraint(a, pltpu.HBM) for a in (snapshots, mean_v, mean_rho, sound)]
    hbm, vmem = pl.BlockSpec(memory_space=pltpu.HBM), pl.BlockSpec(memory_space=pltpu.VMEM)
    return pl.pallas_call(
        outline_kernel,
        out_shape=(
            jax.ShapeDtypeStruct((tiles_n,) + eig_rows.shape, narrow),
            jax.ShapeDtypeStruct((fields + 1, nx, modes), narrow),
            jax.ShapeDtypeStruct((fields, nx, modes), narrow),
            jax.ShapeDtypeStruct((fields, ny, modes), narrow),
            jax.ShapeDtypeStruct((fields, ny, modes), narrow),
        ),
        in_specs=[hbm, vmem, hbm, hbm, hbm],
        out_specs=(vmem,) * 5,
        scratch_shapes=[
            pltpu.VMEM((fields, nx, strip, modes), narrow),
            pltpu.VMEM((fields, nx, strip, modes), narrow),
            pltpu.VMEM((3, nx, ny), jnp.float32),
            pltpu.SemaphoreType.DMA((7,)),
        ],
        compiler_params=pltpu.CompilerParams(vmem_limit_bytes=8 << 20),
        name="outline",
    )(in_hbm[0], eig_rows, *in_hbm[1:])


def contract(left, right):
    return lax.dot_general(left, right, (((0,), (0,)), ((), ())), preferred_element_type=jnp.float32)


def finish_kernel(
    scale, order, g_ref, raw, ct_ref, head_x, tail_x, from_west, from_east, tail_y, from_north, vt_ref, out_ref
):
    modes = g_ref.shape[0]
    ny = head_x.shape[1]
    nx = tail_y.shape[1]
    total = g_ref[:, 0:modes] + g_ref[:, modes : 2 * modes]

    def side(own, other, column, along, cross, sign):
        half_c, half_rho, half_inverse, half_sound = (sign * c for c in column)
        spread_c = viscosity + half_c
        images = [
            half_c * other(0) + half_rho * other(along),
            spread_c * other(1),
            spread_c * other(2),
            spread_c * other(3),
            half_c * other(4) + half_sound * other(along),
        ]
        images[along] = images[along] + half_inverse * other(4)
        added = None
        for f in range(5):
            high, middle, _ = split(images[f])
            one = contract(own(f), high) + contract(own(f), middle)
            added = one if added is None else added + one
        return added

    def plane(ref):
        return lambda f: ref[f].astype(jnp.float32)

    def column_x(i):
        return tuple(ct_ref[0:ny, j * nx + i : j * nx + i + 1] for j in (0, 2, 4, 5))

    total += side(lambda f: head_x[f], plane(from_west), column_x(0), 1, 2, -1.0)
    total += side(lambda f: tail_x[f], plane(from_east), column_x(nx - 1), 1, 2, 1.0)

    own_column = tuple(raw[j * nx : (j + 1) * nx, ny - 1 : ny] for j in (1, 2, 4, 5))
    packed = from_north[5].astype(jnp.float32)
    other_column = tuple(
        packed[:, 3 * j : 3 * j + 1] + packed[:, 3 * j + 1 : 3 * j + 2] + packed[:, 3 * j + 2 : 3 * j + 3]
        for j in range(4)
    )
    total += side(lambda f: tail_y[f], plane(from_north), own_column, 2, 1, 1.0)
    total += side(lambda f: from_north[f], plane(tail_y), other_column, 2, 1, -1.0)

    vt = vt_ref[...]
    right = None
    for part in split(total):
        one = lax.dot_general(part, vt, (((1,), (1,)), ((), ())), preferred_element_type=jnp.float32)
        right = one if right is None else right + one
    both = None
    for part in split(right):
        one = jnp.dot(vt, part, preferred_element_type=jnp.float32)
        both = one if both is None else both + one
    rows = modes // len(order)
    for place, tile in enumerate(order):
        out_ref[place * rows : (place + 1) * rows] = both[tile * rows : (tile + 1) * rows] * scale


def finish(scale, order, *operands):
    modes = operands[-1].shape[0]
    return pl.pallas_call(
        functools.partial(finish_kernel, scale, order),
        out_shape=jax.ShapeDtypeStruct((modes, modes), jnp.float32),
        in_specs=[pl.BlockSpec(memory_space=pltpu.VMEM)] * len(operands),
        out_specs=pl.BlockSpec(memory_space=pltpu.VMEM),
        compiler_params=pltpu.CompilerParams(vmem_limit_bytes=12 << 20),
        name="finish",
    )(*operands)


def body(snapshots, eig_columns, mean_u, mean_v, mean_rho, mean_shear, sound):
    sections = lax.axis_size("sec")
    tiles_n = lax.axis_size("tile")
    fields, nx, ny, modes = snapshots.shape
    rows = modes // tiles_n
    scale = float(fields * nx * ny * sections * tiles_n) ** (-0.5)

    own, head_y, tail_y, head_x, tail_x = outline(
        snapshots, eig_columns.T, tiles_n, mean_v, mean_rho, sound
    )
    vt = lax.all_to_all(own, "tile", 0, 0, tiled=True).reshape(modes, modes)
    from_north = lax.ppermute(head_y, "tile", [(i + 1, i) for i in range(tiles_n - 1)])
    from_west = lax.ppermute(tail_x, "sec", [(i, i + 1) for i in range(sections - 1)])
    from_east = lax.ppermute(head_x, "sec", [(i + 1, i) for i in range(sections - 1)])

    gram, raw, columns = interior(snapshots, mean_u, mean_v, mean_rho, mean_shear, sound)
    far = 4
    near = tiles_n // far
    plane_groups = [[t for t in range(tiles_n) if t // 2 % far == z] for z in range(far)]
    line_groups = [[plane_groups[z][r] for z in range(far)] for r in range(near)]
    order = [t for line in line_groups for t in line]
    local = finish(
        scale, order, gram, raw, columns, head_x, tail_x, from_west, from_east, tail_y, from_north, vt
    )
    shares = lax.all_to_all(
        local.reshape(near, far * rows, modes), "tile", 0, 0, tiled=True, axis_index_groups=plane_groups
    ).sum(0)
    term = lax.all_to_all(
        shares.reshape(far, rows, modes), "tile", 0, 0, tiled=True, axis_index_groups=line_groups
    ).sum(0)
    terms = lax.all_to_all(
        jnp.broadcast_to(term[None], (sections, rows, modes)), "sec", 0, 0, tiled=True
    )
    upstream = jnp.arange(sections) <= lax.axis_index("sec")
    return jnp.where(upstream[:, None, None], terms, 0.0).sum(0)[None]


def solution(mesh):
    in_specs = (
        P(None, "sec", "tile", None),
        P(None, "tile"),
        P("sec", "tile"),
        P("sec", "tile"),
        P("sec", "tile"),
        P("sec", "tile"),
        P("sec", "tile"),
    )
    out_specs = P("sec", "tile", None)
    return jax.shard_map(body, mesh=mesh, in_specs=in_specs, out_specs=out_specs, check_vma=False)
```

```python
import functools

import jax
import jax.numpy as jnp
from jax import lax
from jax.experimental import pallas as pl
from jax.experimental.pallas import tpu as pltpu
from jax.sharding import PartitionSpec as P


viscosity = 0.002
pad = 8
strip = 16


def interior_kernel(x_hbm, mu_hbm, mv_hbm, mr_hbm, ms_hbm, mc_hbm, g_ref, raw, ct_ref, xb, qf, means, image, sems):
    fields, nx, ny, modes = x_hbm.shape

    def copy(i):
        return pltpu.make_async_copy(x_hbm.at[:, i], xb.at[i], sems.at[i])

    coefficients = [
        pltpu.make_async_copy(ref, means.at[j], sems.at[nx + j])
        for j, ref in enumerate((mu_hbm, mv_hbm, mr_hbm, ms_hbm, mc_hbm))
    ]
    for one in coefficients:
        one.start()
    for i in range(nx):
        copy(i).start()

    raw[...] = jnp.zeros_like(raw)
    for one in coefficients:
        one.wait()
    u, v, rho, shear_u, stiff = (means[j] for j in range(5))
    for j, value in enumerate((u * -0.5, v * -0.5, rho * -0.5, -shear_u, -0.5 / rho, stiff * -0.5)):
        raw[j * nx : (j + 1) * nx, 0:ny] = value
    ct_ref[...] = raw[...].T
    qf[0] = jnp.zeros(qf.shape[1:], jnp.float32)
    qf[nx + 1] = jnp.zeros(qf.shape[1:], jnp.float32)
    g_ref[...] = jnp.zeros_like(g_ref)

    def widen(i):
        copy(i).wait()
        edge = jnp.zeros((pad, modes), jnp.float32)
        for f in range(fields):
            qf[i + 1, f, 0:pad] = edge
            qf[i + 1, f, pad + ny : 2 * pad + ny] = edge
            for y in range(0, ny, strip):
                qf[i + 1, f, pad + y : pad + y + strip] = xb[i, f, y : y + strip].astype(jnp.float32)

    def apply(i):
        turned = pltpu.roll(ct_ref[...], 128 - i, 1)
        for y in range(0, ny, strip):
            column = turned[y : y + strip]
            half_u, half_v, half_rho, shear, half_inverse, half_sound = (
                jnp.broadcast_to(column[:, j * nx : j * nx + 1], (strip, modes)) for j in range(6)
            )
            east_c, west_c = viscosity + half_u, viscosity - half_u
            north_c, south_c = viscosity + half_v, viscosity - half_v
            top = pad + y

            def east(f):
                return qf[i + 2, f, top : top + strip]

            def west(f):
                return qf[i, f, top : top + strip]

            def north(f):
                return qf[i + 1, f, top + 1 : top + 1 + strip]

            def south(f):
                return qf[i + 1, f, top - 1 : top - 1 + strip]

            def here(f):
                return qf[i + 1, f, top : top + strip]

            def flow(f):
                return half_u * (east(f) - west(f)) + half_v * (north(f) - south(f))

            def spread(f):
                return (
                    east_c * east(f) + west_c * west(f) + north_c * north(f) + south_c * south(f)
                ) - (4.0 * viscosity) * here(f)

            diverge = (east(1) - west(1)) + (north(2) - south(2))
            images = (
                flow(0) + half_rho * diverge,
                spread(1) + shear * here(2) + half_inverse * (east(4) - west(4)),
                spread(2) + half_inverse * (north(4) - south(4)),
                spread(3),
                flow(4) + half_sound * diverge,
            )
            for f in range(fields):
                high = images[f].astype(jnp.bfloat16)
                low = (images[f] - high.astype(jnp.float32)).astype(jnp.bfloat16)
                image[f * ny + y : f * ny + y + strip, 0:modes] = high
                image[f * ny + y : f * ny + y + strip, modes : 2 * modes] = low
        g_ref[...] += lax.dot_general(
            xb[i].reshape(fields * ny, modes),
            image[...],
            (((0,), (0,)), ((), ())),
            preferred_element_type=jnp.float32,
        )

    widen(0)

    def step(i, carry):
        @pl.when(i + 1 < nx)
        def _():
            widen(i + 1)

        apply(i)
        return carry

    lax.fori_loop(0, nx, step, 0)


def interior(snapshots, *means):
    fields, nx, ny, modes = snapshots.shape
    return pl.pallas_call(
        interior_kernel,
        out_shape=(
            jax.ShapeDtypeStruct((modes, 2 * modes), jnp.float32),
            jax.ShapeDtypeStruct((128, 128), jnp.float32),
            jax.ShapeDtypeStruct((128, 128), jnp.float32),
        ),
        in_specs=[pl.BlockSpec(memory_space=pltpu.HBM)] * 6,
        out_specs=(pl.BlockSpec(memory_space=pltpu.VMEM),) * 3,
        scratch_shapes=[
            pltpu.VMEM((nx, fields, ny, modes), jnp.bfloat16),
            pltpu.VMEM((nx + 2, fields, ny + 2 * pad, modes), jnp.float32),
            pltpu.VMEM((5, nx, ny), jnp.float32),
            pltpu.VMEM((fields * ny, 2 * modes), jnp.bfloat16),
            pltpu.SemaphoreType.DMA((nx + 5,)),
        ],
        compiler_params=pltpu.CompilerParams(vmem_limit_bytes=20 << 20),
        cost_estimate=pl.CostEstimate(flops=20 * 10**9, transcendentals=0, bytes_accessed=10**7),
        name="interior",
    )(*(pltpu.with_memory_space_constraint(a, pltpu.HBM) for a in (snapshots, *means)))


def split(value):
    high = value.astype(jnp.bfloat16)
    rest = value - high.astype(jnp.float32)
    middle = rest.astype(jnp.bfloat16)
    return high, middle, (rest - middle.astype(jnp.float32)).astype(jnp.bfloat16)


def repeat_kernel(eig_hbm, own_ref, held, sem):
    copy = pltpu.make_async_copy(eig_hbm, held, sem)
    copy.start()
    copy.wait()
    for t in range(own_ref.shape[0]):
        own_ref[t] = held[...]


def repeat(eig_rows, times):
    return pl.pallas_call(
        repeat_kernel,
        out_shape=jax.ShapeDtypeStruct((times,) + eig_rows.shape, eig_rows.dtype),
        in_specs=[pl.BlockSpec(memory_space=pltpu.HBM)],
        out_specs=pl.BlockSpec(memory_space=pltpu.VMEM),
        scratch_shapes=[pltpu.VMEM(eig_rows.shape, eig_rows.dtype), pltpu.SemaphoreType.DMA],
        compiler_params=pltpu.CompilerParams(vmem_limit_bytes=2 << 20),
        name="repeat",
    )(pltpu.with_memory_space_constraint(eig_rows, pltpu.HBM))


def outline_kernel(x_hbm, mv_hbm, mr_hbm, mc_hbm, head_y, tail_y, head_x, tail_x, low, high, means, sems):
    fields, nx, ny, modes = x_hbm.shape
    copies = [
        pltpu.make_async_copy(x_hbm.at[:, :, 0:strip], low, sems.at[0]),
        pltpu.make_async_copy(x_hbm.at[:, :, ny - strip : ny], high, sems.at[1]),
        pltpu.make_async_copy(x_hbm.at[:, 0], head_x, sems.at[2]),
        pltpu.make_async_copy(x_hbm.at[:, nx - 1], tail_x, sems.at[3]),
        pltpu.make_async_copy(mv_hbm, means.at[0], sems.at[4]),
        pltpu.make_async_copy(mr_hbm, means.at[1], sems.at[5]),
        pltpu.make_async_copy(mc_hbm, means.at[2], sems.at[6]),
    ]
    for copy in copies:
        copy.start()
    rows = lax.broadcasted_iota(jnp.int32, (nx, nx * strip), 0)
    cells = lax.broadcasted_iota(jnp.int32, (nx, nx * strip), 1)
    lanes = lax.broadcasted_iota(jnp.int32, (nx, modes), 1)
    for at, held, source, edge in ((0, low, head_y, 0), (1, high, tail_y, strip - 1)):
        chosen = jnp.where(cells == rows * strip + edge, 1.0, 0.0).astype(jnp.bfloat16)
        copies[at].wait()
        for f in range(fields):
            picked = jnp.dot(
                chosen, held[f].reshape(nx * strip, modes), preferred_element_type=jnp.float32
            )
            source[f] = picked.astype(jnp.bfloat16)
    for copy in copies[4:]:
        copy.wait()
    v, rho, stiff = (means[j, :, 0:1] for j in range(3))
    packed = jnp.zeros((nx, modes), jnp.float32)
    for j, value in enumerate((v * -0.5, rho * -0.5, -0.5 / rho, stiff * -0.5)):
        for p, part in enumerate(split(value)):
            packed = jnp.where(lanes == 3 * j + p, part.astype(jnp.float32), packed)
    head_y[fields] = packed.astype(jnp.bfloat16)
    copies[2].wait()
    copies[3].wait()


def outline(snapshots, mean_v, mean_rho, sound):
    fields, nx, ny, modes = snapshots.shape
    narrow = jnp.bfloat16
    in_hbm = [pltpu.with_memory_space_constraint(a, pltpu.HBM) for a in (snapshots, mean_v, mean_rho, sound)]
    hbm, vmem = pl.BlockSpec(memory_space=pltpu.HBM), pl.BlockSpec(memory_space=pltpu.VMEM)
    return pl.pallas_call(
        outline_kernel,
        out_shape=(
            jax.ShapeDtypeStruct((fields + 1, nx, modes), narrow),
            jax.ShapeDtypeStruct((fields, nx, modes), narrow),
            jax.ShapeDtypeStruct((fields, ny, modes), narrow),
            jax.ShapeDtypeStruct((fields, ny, modes), narrow),
        ),
        in_specs=[hbm] * 4,
        out_specs=(vmem,) * 4,
        scratch_shapes=[
            pltpu.VMEM((fields, nx, strip, modes), narrow),
            pltpu.VMEM((fields, nx, strip, modes), narrow),
            pltpu.VMEM((3, nx, ny), jnp.float32),
            pltpu.SemaphoreType.DMA((7,)),
        ],
        compiler_params=pltpu.CompilerParams(vmem_limit_bytes=8 << 20),
        name="outline",
    )(*in_hbm)


def contract(left, right):
    return lax.dot_general(left, right, (((0,), (0,)), ((), ())), preferred_element_type=jnp.float32)


def finish_kernel(
    scale, gathered, order, g_ref, raw, ct_ref, head_x, tail_x, from_west, from_east, tail_y, from_north, vt_ref, out_ref, placed
):
    modes = g_ref.shape[0]
    ny = head_x.shape[1]
    nx = tail_y.shape[1]
    total = g_ref[:, 0:modes] + g_ref[:, modes : 2 * modes]

    def side(own, other, column, along, sign):
        half_c, half_rho, half_inverse, half_sound = (sign * c for c in column)
        spread_c = viscosity + half_c
        images = [
            half_c * other(0) + half_rho * other(along),
            spread_c * other(1),
            spread_c * other(2),
            spread_c * other(3),
            half_c * other(4) + half_sound * other(along),
        ]
        images[along] = images[along] + half_inverse * other(4)
        added = None
        for f in range(5):
            high, middle, _ = split(images[f])
            one = contract(own(f), high) + contract(own(f), middle)
            added = one if added is None else added + one
        return added

    def plane(ref):
        return lambda f: ref[f].astype(jnp.float32)

    def column_x(i):
        return tuple(ct_ref[0:ny, j * nx + i : j * nx + i + 1] for j in (0, 2, 4, 5))

    total += side(lambda f: head_x[f], plane(from_west), column_x(0), 1, -1.0)
    total += side(lambda f: tail_x[f], plane(from_east), column_x(nx - 1), 1, 1.0)

    own_column = tuple(raw[j * nx : (j + 1) * nx, ny - 1 : ny] for j in (1, 2, 4, 5))
    packed = from_north[5].astype(jnp.float32)
    other_column = tuple(
        packed[:, 3 * j : 3 * j + 1] + packed[:, 3 * j + 1 : 3 * j + 2] + packed[:, 3 * j + 2 : 3 * j + 3]
        for j in range(4)
    )
    total += side(lambda f: tail_y[f], plane(from_north), own_column, 2, 1.0)
    total += side(lambda f: from_north[f], plane(tail_y), other_column, 2, -1.0)

    rows = modes // len(order)
    for place, tile in enumerate(gathered):
        placed[tile * rows : (tile + 1) * rows] = vt_ref[place].astype(jnp.float32)
    vt = placed[...].astype(jnp.bfloat16)
    right = None
    for part in split(total):
        one = lax.dot_general(part, vt, (((1,), (1,)), ((), ())), preferred_element_type=jnp.float32)
        right = one if right is None else right + one
    both = None
    for part in split(right):
        one = jnp.dot(vt, part, preferred_element_type=jnp.float32)
        both = one if both is None else both + one
    for place, tile in enumerate(order):
        out_ref[place * rows : (place + 1) * rows] = both[tile * rows : (tile + 1) * rows] * scale


def finish(scale, gathered, order, *operands):
    modes = operands[-1].shape[-1]
    return pl.pallas_call(
        functools.partial(finish_kernel, scale, gathered, order),
        out_shape=jax.ShapeDtypeStruct((modes, modes), jnp.float32),
        in_specs=[pl.BlockSpec(memory_space=pltpu.VMEM)] * len(operands),
        out_specs=pl.BlockSpec(memory_space=pltpu.VMEM),
        scratch_shapes=[pltpu.VMEM((modes, modes), jnp.float32)],
        compiler_params=pltpu.CompilerParams(vmem_limit_bytes=12 << 20),
        name="finish",
    )(*operands)


def body(snapshots, eig_columns, mean_u, mean_v, mean_rho, mean_shear, sound):
    sections = lax.axis_size("sec")
    tiles_n = lax.axis_size("tile")
    fields, nx, ny, modes = snapshots.shape
    rows = modes // tiles_n
    scale = float(fields * nx * ny * sections * tiles_n) ** (-0.5)

    far = 4
    near = tiles_n // far
    wide = near // 2
    gathered = [
        ((x + wide // 2) % wide * far + (z + far // 2) % far) * 2 + core
        for x in range(wide)
        for z in range(far)
        for core in range(2)
    ]
    arrived = [(s + sections - 2) % sections for s in range(sections)]
    own = repeat(eig_columns.T, tiles_n)
    vt = lax.all_to_all(own, "tile", 0, 0, tiled=True, axis_index_groups=[gathered])
    head_y, tail_y, head_x, tail_x = outline(snapshots, mean_v, mean_rho, sound)
    from_north = lax.ppermute(head_y, "tile", [(i + 1, i) for i in range(tiles_n - 1)])
    from_west = lax.ppermute(tail_x, "sec", [(i, i + 1) for i in range(sections - 1)])
    from_east = lax.ppermute(head_x, "sec", [(i + 1, i) for i in range(sections - 1)])

    gram, raw, columns = interior(snapshots, mean_u, mean_v, mean_rho, mean_shear, sound)
    plane_groups = [[t for t in range(tiles_n) if t // 2 % far == (z + far // 2) % far] for z in range(far)]
    line_groups = [[plane_groups[z][r] for z in range(far)] for r in range(near)]
    order = [t for line in line_groups for t in line]
    local = finish(
        scale, gathered, order, gram, raw, columns, head_x, tail_x, from_west, from_east, tail_y, from_north, vt
    )
    shares = lax.all_to_all(
        local.reshape(near, far * rows, modes), "tile", 0, 0, tiled=True, axis_index_groups=plane_groups
    ).sum(0)
    term = lax.all_to_all(
        shares.reshape(far, rows, modes), "tile", 0, 0, tiled=True, axis_index_groups=line_groups
    ).sum(0)
    terms = lax.all_to_all(
        jnp.broadcast_to(term[None], (sections, rows, modes)), "sec", 0, 0, tiled=True, axis_index_groups=[arrived]
    )
    upstream = jnp.array(arrived) <= lax.axis_index("sec")
    return jnp.where(upstream[:, None, None], terms, 0.0).sum(0)[None]


def solution(mesh):
    in_specs = (
        P(None, "sec", "tile", None),
        P(None, "tile"),
        P("sec", "tile"),
        P("sec", "tile"),
        P("sec", "tile"),
        P("sec", "tile"),
        P("sec", "tile"),
    )
    out_specs = P("sec", "tile", None)
    return jax.shard_map(body, mesh=mesh, in_specs=in_specs, out_specs=out_specs, check_vma=False)
```

```python
import functools

import jax
import jax.numpy as jnp
from jax import lax
from jax.experimental import pallas as pl
from jax.experimental.pallas import tpu as pltpu
from jax.sharding import PartitionSpec as P


viscosity = 0.002
pad = 8
strip = 16
lanes = 128


def interior_kernel(
    x_hbm, mu_hbm, mv_hbm, mr_hbm, ms_hbm, mc_hbm, g_ref, raw, ct_ref, xb, qf, means, even, odd, sems
):
    fields, nx, ny, modes = x_hbm.shape
    halves = modes // lanes

    def copy(i):
        return pltpu.make_async_copy(x_hbm.at[:, i], xb.at[i], sems.at[i])

    coefficients = [
        pltpu.make_async_copy(ref, means.at[j], sems.at[nx + j])
        for j, ref in enumerate((mu_hbm, mv_hbm, mr_hbm, ms_hbm, mc_hbm))
    ]
    for one in coefficients:
        one.start()
    for i in range(nx):
        copy(i).start()

    raw[...] = jnp.zeros_like(raw)
    qf[0] = jnp.zeros(qf.shape[1:], jnp.float32)
    odd[...] = jnp.zeros_like(odd)
    g_ref[...] = jnp.zeros_like(g_ref)
    for one in coefficients:
        one.wait()
    u, v, rho, shear_u, stiff = (means[j] for j in range(5))
    for j, value in enumerate((u * -0.5, v * -0.5, rho * -0.5, -shear_u, -0.5 / rho, stiff * -0.5)):
        raw[j * nx : (j + 1) * nx, 0:ny] = value
    ct_ref[...] = raw[...].T

    def widen(i):
        edge = jnp.zeros((pad, lanes), jnp.float32)
        for f in range(fields):
            for h in range(halves):
                part = slice(h * lanes, (h + 1) * lanes)
                qf[i + 1, f, h, 0:pad] = edge
                qf[i + 1, f, h, pad + ny : 2 * pad + ny] = edge
                for y in range(0, ny, strip):
                    qf[i + 1, f, h, pad + y : pad + y + strip] = xb[i, f, y : y + strip, part].astype(
                        jnp.float32
                    )

    def apply(i, image):
        zero = jnp.minimum(i, 0)
        turned = pltpu.roll(ct_ref[...], 128 - i, 1)
        for y in range(0, ny, strip):
            column = turned[y : y + strip]
            half_u, half_v, half_rho, shear, half_inverse, half_sound = (
                jnp.broadcast_to(column[:, j * nx : j * nx + 1], (strip, lanes)) for j in range(6)
            )
            east_c, west_c = viscosity + half_u, viscosity - half_u
            north_c, south_c = viscosity + half_v, viscosity - half_v
            top = pad + y
            for h in range(halves):

                def east(f):
                    return qf[i + 2, f, h, top : top + strip]

                def west(f):
                    return qf[i, f, h, top : top + strip]

                def north(f):
                    return qf[i + 1, f, h, pl.ds(zero + top + 1, strip)]

                def south(f):
                    return qf[i + 1, f, h, pl.ds(zero + top - 1, strip)]

                def here(f):
                    return qf[i + 1, f, h, top : top + strip]

                def flow(f):
                    return half_u * (east(f) - west(f)) + half_v * (north(f) - south(f))

                def spread(f):
                    return (
                        east_c * east(f) + west_c * west(f) + north_c * north(f) + south_c * south(f)
                    ) - (4.0 * viscosity) * here(f)

                diverge = (east(1) - west(1)) + (north(2) - south(2))
                images = (
                    flow(0) + half_rho * diverge,
                    spread(1) + shear * here(2) + half_inverse * (east(4) - west(4)),
                    spread(2) + half_inverse * (north(4) - south(4)),
                    spread(3),
                    flow(4) + half_sound * diverge,
                )
                for f in range(fields):
                    high = images[f].astype(jnp.bfloat16)
                    row = f * ny + y
                    image[row : row + strip, h * lanes : (h + 1) * lanes] = high

    def gather(i, image):
        g_ref[...] += lax.dot_general(
            xb[i].reshape(fields * ny, modes),
            image[...],
            (((0,), (0,)), ((), ())),
            preferred_element_type=jnp.float32,
        )

    copy(0).wait()
    widen(0)

    def step(p, carry):
        i = 2 * p
        copy(i + 1).wait()
        widen(i + 1)
        apply(i, even)
        gather(jnp.maximum(i - 1, 0), odd)

        @pl.when(i + 2 < nx)
        def _():
            copy(i + 2).wait()
            widen(i + 2)

        @pl.when(i + 2 == nx)
        def _():
            qf[nx + 1] = jnp.zeros(qf.shape[1:], jnp.float32)

        apply(i + 1, odd)
        gather(i, even)
        return carry

    lax.fori_loop(0, nx // 2, step, 0)
    gather(nx - 1, odd)


def interior(snapshots, *means):
    fields, nx, ny, modes = snapshots.shape
    return pl.pallas_call(
        interior_kernel,
        out_shape=(
            jax.ShapeDtypeStruct((modes, modes), jnp.float32),
            jax.ShapeDtypeStruct((128, 128), jnp.float32),
            jax.ShapeDtypeStruct((128, 128), jnp.float32),
        ),
        in_specs=[pl.BlockSpec(memory_space=pltpu.HBM)] * 6,
        out_specs=(pl.BlockSpec(memory_space=pltpu.VMEM),) * 3,
        scratch_shapes=[
            pltpu.VMEM((nx, fields, ny, modes), jnp.bfloat16),
            pltpu.VMEM((nx + 2, fields, modes // lanes, ny + 2 * pad, lanes), jnp.float32),
            pltpu.VMEM((5, nx, ny), jnp.float32),
            pltpu.VMEM((fields * ny, modes), jnp.bfloat16),
            pltpu.VMEM((fields * ny, modes), jnp.bfloat16),
            pltpu.SemaphoreType.DMA((nx + 5,)),
        ],
        compiler_params=pltpu.CompilerParams(vmem_limit_bytes=20 << 20),
        cost_estimate=pl.CostEstimate(flops=20 * 10**9, transcendentals=0, bytes_accessed=10**7),
        name="interior",
    )(*(pltpu.with_memory_space_constraint(a, pltpu.HBM) for a in (snapshots, *means)))


def split(value):
    high = value.astype(jnp.bfloat16)
    rest = value - high.astype(jnp.float32)
    middle = rest.astype(jnp.bfloat16)
    return high, middle, (rest - middle.astype(jnp.float32)).astype(jnp.bfloat16)


def outline_kernel(
    x_hbm, eig_hbm, mv_hbm, mr_hbm, mc_hbm, own_ref, head_y, tail_y, head_x, tail_x, low, high, means, rows_ref, sems
):
    fields, nx, ny, modes = x_hbm.shape
    copies = [
        pltpu.make_async_copy(x_hbm.at[:, :, 0:strip], low, sems.at[0]),
        pltpu.make_async_copy(x_hbm.at[:, :, ny - strip : ny], high, sems.at[1]),
        pltpu.make_async_copy(x_hbm.at[:, 0], head_x, sems.at[2]),
        pltpu.make_async_copy(x_hbm.at[:, nx - 1], tail_x, sems.at[3]),
        pltpu.make_async_copy(mv_hbm, means.at[0], sems.at[4]),
        pltpu.make_async_copy(mr_hbm, means.at[1], sems.at[5]),
        pltpu.make_async_copy(mc_hbm, means.at[2], sems.at[6]),
    ]
    copies.append(pltpu.make_async_copy(eig_hbm, rows_ref, sems.at[7]))
    for copy in [copies[7]] + copies[:7]:
        copy.start()
    copies[7].wait()
    for t in range(own_ref.shape[0]):
        own_ref[t] = rows_ref[...]
    rows = lax.broadcasted_iota(jnp.int32, (nx, nx * strip), 0)
    cells = lax.broadcasted_iota(jnp.int32, (nx, nx * strip), 1)
    places = lax.broadcasted_iota(jnp.int32, (nx, modes), 1)
    for at, held, source, edge in ((0, low, head_y, 0), (1, high, tail_y, strip - 1)):
        chosen = jnp.where(cells == rows * strip + edge, 1.0, 0.0).astype(jnp.bfloat16)
        copies[at].wait()
        for f in range(fields):
            picked = jnp.dot(
                chosen, held[f].reshape(nx * strip, modes), preferred_element_type=jnp.float32
            )
            source[f] = picked.astype(jnp.bfloat16)
    for copy in copies[4:7]:
        copy.wait()
    v, rho, stiff = (means[j, :, 0:1] for j in range(3))
    packed = jnp.zeros((nx, modes), jnp.float32)
    for j, value in enumerate((v * -0.5, rho * -0.5, -0.5 / rho, stiff * -0.5)):
        for p, part in enumerate(split(value)):
            packed = jnp.where(places == 3 * j + p, part.astype(jnp.float32), packed)
    head_y[fields] = packed.astype(jnp.bfloat16)
    for copy in copies[2:4]:
        copy.wait()


def outline(snapshots, eig_rows, tiles_n, mean_v, mean_rho, sound):
    fields, nx, ny, modes = snapshots.shape
    narrow = jnp.bfloat16
    in_hbm = [pltpu.with_memory_space_constraint(a, pltpu.HBM) for a in (snapshots, eig_rows, mean_v, mean_rho, sound)]
    hbm, vmem = pl.BlockSpec(memory_space=pltpu.HBM), pl.BlockSpec(memory_space=pltpu.VMEM)
    return pl.pallas_call(
        outline_kernel,
        out_shape=(
            jax.ShapeDtypeStruct((tiles_n,) + eig_rows.shape, narrow),
            jax.ShapeDtypeStruct((fields + 1, nx, modes), narrow),
            jax.ShapeDtypeStruct((fields, nx, modes), narrow),
            jax.ShapeDtypeStruct((fields, ny, modes), narrow),
            jax.ShapeDtypeStruct((fields, ny, modes), narrow),
        ),
        in_specs=[hbm] * 5,
        out_specs=(vmem,) * 5,
        scratch_shapes=[
            pltpu.VMEM((fields, nx, strip, modes), narrow),
            pltpu.VMEM((fields, nx, strip, modes), narrow),
            pltpu.VMEM((3, nx, ny), jnp.float32),
            pltpu.VMEM(eig_rows.shape, narrow),
            pltpu.SemaphoreType.DMA((8,)),
        ],
        compiler_params=pltpu.CompilerParams(vmem_limit_bytes=8 << 20),
        name="outline",
    )(*in_hbm)


def contract(left, right):
    return lax.dot_general(left, right, (((0,), (0,)), ((), ())), preferred_element_type=jnp.float32)


def finish_kernel(
    scale, gathered, order, g_ref, raw, ct_ref, head_x, tail_x, from_west, from_east, tail_y, from_north, vt_ref, out_ref, placed, image
):
    modes = g_ref.shape[0]
    ny = head_x.shape[1]
    nx = tail_y.shape[1]
    total = g_ref[...]

    def side(own, other, column, along, sign):
        half_c, half_rho, half_inverse, half_sound = (sign * c for c in column)
        spread_c = viscosity + half_c
        images = [
            half_c * other(0) + half_rho * other(along),
            spread_c * other(1),
            spread_c * other(2),
            spread_c * other(3),
            half_c * other(4) + half_sound * other(along),
        ]
        images[along] = images[along] + half_inverse * other(4)
        size = own.shape[1]
        for f in range(5):
            image[f * size : (f + 1) * size] = images[f].astype(jnp.bfloat16)
        return contract(own[0:5].reshape(5 * size, modes), image[0 : 5 * size])

    def plane(ref):
        return lambda f: ref[f].astype(jnp.float32)

    def column_x(i):
        return tuple(ct_ref[0:ny, j * nx + i : j * nx + i + 1] for j in (0, 2, 4, 5))

    total += side(head_x, plane(from_west), column_x(0), 1, -1.0)
    total += side(tail_x, plane(from_east), column_x(nx - 1), 1, 1.0)
    own_column = tuple(raw[j * nx : (j + 1) * nx, ny - 1 : ny] for j in (1, 2, 4, 5))
    packed = from_north[5].astype(jnp.float32)
    other_column = tuple(
        packed[:, 3 * j : 3 * j + 1] + packed[:, 3 * j + 1 : 3 * j + 2] + packed[:, 3 * j + 2 : 3 * j + 3]
        for j in range(4)
    )
    total += side(tail_y, plane(from_north), own_column, 2, 1.0)
    total += side(from_north, plane(tail_y), other_column, 2, -1.0)

    rows = modes // len(order)
    for place, tile in enumerate(gathered):
        placed[tile * rows : (tile + 1) * rows] = vt_ref[place].astype(jnp.float32)
    vt = placed[...].astype(jnp.bfloat16)
    right = None
    for part in split(total)[:2]:
        one = lax.dot_general(part, vt, (((1,), (1,)), ((), ())), preferred_element_type=jnp.float32)
        right = one if right is None else right + one
    both = None
    for part in split(right)[:2]:
        one = jnp.dot(vt, part, preferred_element_type=jnp.float32)
        both = one if both is None else both + one
    for place, tile in enumerate(order):
        out_ref[place] = (both[tile * rows : (tile + 1) * rows] * scale).astype(jnp.bfloat16)


def finish(scale, gathered, order, *operands):
    modes = operands[-1].shape[-1]
    return pl.pallas_call(
        functools.partial(finish_kernel, scale, gathered, order),
        out_shape=jax.ShapeDtypeStruct((len(order), modes // len(order), modes), jnp.bfloat16),
        in_specs=[pl.BlockSpec(memory_space=pltpu.VMEM)] * len(operands),
        out_specs=pl.BlockSpec(memory_space=pltpu.VMEM),
        scratch_shapes=[
            pltpu.VMEM((modes, modes), jnp.float32),
            pltpu.VMEM((480, modes), jnp.bfloat16),
        ],
        compiler_params=pltpu.CompilerParams(vmem_limit_bytes=12 << 20),
        name="finish",
    )(*operands)


def body(snapshots, eig_columns, mean_u, mean_v, mean_rho, mean_shear, sound):
    sections = lax.axis_size("sec")
    tiles_n = lax.axis_size("tile")
    fields, nx, ny, modes = snapshots.shape
    rows = modes // tiles_n
    scale = float(fields * nx * ny * sections * tiles_n) ** (-0.5)

    far = 4
    near = tiles_n // far
    wide = near // 2
    gathered = [
        ((x + wide // 2) % wide * far + (z + far // 2) % far) * 2 + core
        for x in range(wide)
        for z in range(far)
        for core in range(2)
    ]
    arrived = [(s + sections - 2) % sections for s in range(sections)]
    own, head_y, tail_y, head_x, tail_x = outline(
        snapshots, eig_columns.T, tiles_n, mean_v, mean_rho, sound
    )
    vt = lax.all_to_all(own, "tile", 0, 0, tiled=True, axis_index_groups=[gathered])
    from_north = lax.ppermute(head_y, "tile", [(i + 1, i) for i in range(tiles_n - 1)])
    from_west = lax.ppermute(tail_x, "sec", [(i, i + 1) for i in range(sections - 1)])
    from_east = lax.ppermute(head_x, "sec", [(i + 1, i) for i in range(sections - 1)])

    gram, raw, columns = interior(snapshots, mean_u, mean_v, mean_rho, mean_shear, sound)
    local = finish(
        scale, gathered, gathered, gram, raw, columns, head_x, tail_x, from_west, from_east, tail_y, from_north, vt
    )
    shares = lax.all_to_all(local, "tile", 0, 0, tiled=True, axis_index_groups=[gathered])
    term = shares.astype(jnp.float32).sum(0)
    terms = lax.all_to_all(
        jnp.broadcast_to(term[None], (sections, rows, modes)), "sec", 0, 0, tiled=True, axis_index_groups=[arrived]
    )
    upstream = jnp.array(arrived) <= lax.axis_index("sec")
    return jnp.where(upstream[:, None, None], terms, 0.0).sum(0)[None]


def solution(mesh):
    in_specs = (
        P(None, "sec", "tile", None),
        P(None, "tile"),
        P("sec", "tile"),
        P("sec", "tile"),
        P("sec", "tile"),
        P("sec", "tile"),
        P("sec", "tile"),
    )
    out_specs = P("sec", "tile", None)
    return jax.shard_map(body, mesh=mesh, in_specs=in_specs, out_specs=out_specs, check_vma=False)
```

```python
import functools

import jax
import jax.numpy as jnp
from jax import lax
from jax.experimental import pallas as pl
from jax.experimental.pallas import tpu as pltpu
from jax.sharding import PartitionSpec as P


viscosity = 0.002
pad = 8
strip = 16
lanes = 128
period = 4


def interior_kernel(
    x_hbm, mu_hbm, mv_hbm, mr_hbm, ms_hbm, mc_hbm, g_ref, raw, ct_ref, xb, q0, q1, q2, q3, means, i0, i1, sems
):
    fields, nx, ny, modes = x_hbm.shape
    halves = modes // lanes

    def copy(i):
        return pltpu.make_async_copy(x_hbm.at[:, i], xb.at[i], sems.at[i])

    coefficients = [
        pltpu.make_async_copy(ref, means.at[j], sems.at[nx + j])
        for j, ref in enumerate((mu_hbm, mv_hbm, mr_hbm, ms_hbm, mc_hbm))
    ]
    for one in coefficients:
        one.start()
    for i in range(nx):
        copy(i).start()

    ring, image_ring = (q0, q1, q2, q3), (i0, i1)
    edge = jnp.zeros((pad, lanes), jnp.float32)
    raw[...] = jnp.zeros_like(raw)
    for plane in ring:
        for f in range(fields):
            for h in range(halves):
                plane[f, h, 0:pad] = edge
                plane[f, h, pad + ny : 2 * pad + ny] = edge
    q3[...] = jnp.zeros_like(q3)
    i1[...] = jnp.zeros_like(i1)
    xb[nx] = jnp.zeros(xb.shape[1:], xb.dtype)
    xb[nx + 1] = jnp.zeros(xb.shape[1:], xb.dtype)
    g_ref[...] = jnp.zeros_like(g_ref)
    for one in coefficients:
        one.wait()
    u, v, rho, shear_u, stiff = (means[j] for j in range(5))
    for j, value in enumerate((u * -0.5, v * -0.5, rho * -0.5, -shear_u, -0.5 / rho, stiff * -0.5)):
        raw[j * nx : (j + 1) * nx, 0:ny] = value
    ct_ref[...] = raw[...].T

    def widen(i, plane):
        for f in range(fields):
            for h in range(halves):
                part = slice(h * lanes, (h + 1) * lanes)
                for y in range(0, ny, strip):
                    plane[f, h, pad + y : pad + y + strip] = xb[i, f, y : y + strip, part].astype(
                        jnp.float32
                    )

    def apply(i, behind, middle, ahead, image):
        zero = jnp.minimum(i, 0)
        turned = pltpu.roll(ct_ref[...], 128 - i, 1)
        for y in range(0, ny, strip):
            column = turned[y : y + strip]
            half_u, half_v, half_rho, shear, half_inverse, half_sound = (
                jnp.broadcast_to(column[:, j * nx : j * nx + 1], (strip, lanes)) for j in range(6)
            )
            east_c, west_c = viscosity + half_u, viscosity - half_u
            north_c, south_c = viscosity + half_v, viscosity - half_v
            top = pad + y
            for h in range(halves):

                def east(f):
                    return ahead[f, h, top : top + strip]

                def west(f):
                    return behind[f, h, top : top + strip]

                def north(f):
                    return middle[f, h, pl.ds(zero + top + 1, strip)]

                def south(f):
                    return middle[f, h, pl.ds(zero + top - 1, strip)]

                def here(f):
                    return middle[f, h, top : top + strip]

                def flow(f):
                    return half_u * (east(f) - west(f)) + half_v * (north(f) - south(f))

                def spread(f):
                    return (
                        east_c * east(f) + west_c * west(f) + north_c * north(f) + south_c * south(f)
                    ) - (4.0 * viscosity) * here(f)

                diverge = (east(1) - west(1)) + (north(2) - south(2))
                images = (
                    flow(0) + half_rho * diverge,
                    spread(1) + shear * here(2) + half_inverse * (east(4) - west(4)),
                    spread(2) + half_inverse * (north(4) - south(4)),
                    spread(3),
                    flow(4) + half_sound * diverge,
                )
                for f in range(fields):
                    high = images[f].astype(jnp.bfloat16)
                    row = f * ny + y
                    image[row : row + strip, h * lanes : (h + 1) * lanes] = high

    def gather(i, image):
        g_ref[...] += lax.dot_general(
            xb[i].reshape(fields * ny, modes),
            image[...],
            (((0,), (0,)), ((), ())),
            preferred_element_type=jnp.float32,
        )

    for i in range(2):
        copy(i).wait()
        widen(i, ring[i])

    def step(p, carry):
        first = period * p
        for one in range(2, period):
            copy(first + one).wait()

        @pl.when(first + period < nx)
        def _():
            copy(first + period).wait()
            copy(first + period + 1).wait()

        for one in range(period):
            i = first + one
            apply(i, ring[(one - 1) % 4], ring[one], ring[(one + 1) % 4], image_ring[one % 2])
            gather(jnp.maximum(i - 1, 0), image_ring[(one + 1) % 2])
            widen(i + 2, ring[(one + 2) % 4])
        return carry

    lax.fori_loop(0, nx // period, step, 0)
    gather(nx - 1, image_ring[(nx - 1) % 2])


def interior(snapshots, *means):
    fields, nx, ny, modes = snapshots.shape
    return pl.pallas_call(
        interior_kernel,
        out_shape=(
            jax.ShapeDtypeStruct((modes, modes), jnp.float32),
            jax.ShapeDtypeStruct((128, 128), jnp.float32),
            jax.ShapeDtypeStruct((128, 128), jnp.float32),
        ),
        in_specs=[pl.BlockSpec(memory_space=pltpu.HBM)] * 6,
        out_specs=(pl.BlockSpec(memory_space=pltpu.VMEM),) * 3,
        scratch_shapes=[
            pltpu.VMEM((nx + 2, fields, ny, modes), jnp.bfloat16),
            pltpu.VMEM((fields, modes // lanes, ny + 2 * pad, lanes), jnp.float32),
            pltpu.VMEM((fields, modes // lanes, ny + 2 * pad, lanes), jnp.float32),
            pltpu.VMEM((fields, modes // lanes, ny + 2 * pad, lanes), jnp.float32),
            pltpu.VMEM((fields, modes // lanes, ny + 2 * pad, lanes), jnp.float32),
            pltpu.VMEM((5, nx, ny), jnp.float32),
            pltpu.VMEM((fields * ny, modes), jnp.bfloat16),
            pltpu.VMEM((fields * ny, modes), jnp.bfloat16),
            pltpu.SemaphoreType.DMA((nx + 5,)),
        ],
        compiler_params=pltpu.CompilerParams(vmem_limit_bytes=20 << 20),
        cost_estimate=pl.CostEstimate(flops=20 * 10**9, transcendentals=0, bytes_accessed=10**7),
        name="interior",
    )(*(pltpu.with_memory_space_constraint(a, pltpu.HBM) for a in (snapshots, *means)))


def split(value):
    high = value.astype(jnp.bfloat16)
    rest = value - high.astype(jnp.float32)
    middle = rest.astype(jnp.bfloat16)
    return high, middle, (rest - middle.astype(jnp.float32)).astype(jnp.bfloat16)


def outline_kernel(
    x_hbm, eig_hbm, mv_hbm, mr_hbm, mc_hbm, own_ref, head_y, tail_y, head_x, tail_x, low, high, means, rows_ref, sems
):
    fields, nx, ny, modes = x_hbm.shape
    copies = [
        pltpu.make_async_copy(x_hbm.at[:, :, 0:strip], low, sems.at[0]),
        pltpu.make_async_copy(x_hbm.at[:, :, ny - strip : ny], high, sems.at[1]),
        pltpu.make_async_copy(x_hbm.at[:, 0], head_x, sems.at[2]),
        pltpu.make_async_copy(x_hbm.at[:, nx - 1], tail_x, sems.at[3]),
        pltpu.make_async_copy(mv_hbm, means.at[0], sems.at[4]),
        pltpu.make_async_copy(mr_hbm, means.at[1], sems.at[5]),
        pltpu.make_async_copy(mc_hbm, means.at[2], sems.at[6]),
    ]
    copies.append(pltpu.make_async_copy(eig_hbm, rows_ref, sems.at[7]))
    for copy in [copies[7]] + copies[:7]:
        copy.start()
    copies[7].wait()
    for t in range(own_ref.shape[0]):
        own_ref[t] = rows_ref[...]
    rows = lax.broadcasted_iota(jnp.int32, (nx, nx * strip), 0)
    cells = lax.broadcasted_iota(jnp.int32, (nx, nx * strip), 1)
    places = lax.broadcasted_iota(jnp.int32, (nx, modes), 1)
    for at, held, source, edge in ((0, low, head_y, 0), (1, high, tail_y, strip - 1)):
        chosen = jnp.where(cells == rows * strip + edge, 1.0, 0.0).astype(jnp.bfloat16)
        copies[at].wait()
        for f in range(fields):
            picked = jnp.dot(
                chosen, held[f].reshape(nx * strip, modes), preferred_element_type=jnp.float32
            )
            source[f] = picked.astype(jnp.bfloat16)
    for copy in copies[4:7]:
        copy.wait()
    v, rho, stiff = (means[j, :, 0:1] for j in range(3))
    packed = jnp.zeros((nx, modes), jnp.float32)
    for j, value in enumerate((v * -0.5, rho * -0.5, -0.5 / rho, stiff * -0.5)):
        for p, part in enumerate(split(value)):
            packed = jnp.where(places == 3 * j + p, part.astype(jnp.float32), packed)
    head_y[fields] = packed.astype(jnp.bfloat16)
    for copy in copies[2:4]:
        copy.wait()


def outline(snapshots, eig_rows, tiles_n, mean_v, mean_rho, sound):
    fields, nx, ny, modes = snapshots.shape
    narrow = jnp.bfloat16
    in_hbm = [pltpu.with_memory_space_constraint(a, pltpu.HBM) for a in (snapshots, eig_rows, mean_v, mean_rho, sound)]
    hbm, vmem = pl.BlockSpec(memory_space=pltpu.HBM), pl.BlockSpec(memory_space=pltpu.VMEM)
    return pl.pallas_call(
        outline_kernel,
        out_shape=(
            jax.ShapeDtypeStruct((tiles_n,) + eig_rows.shape, narrow),
            jax.ShapeDtypeStruct((fields + 1, nx, modes), narrow),
            jax.ShapeDtypeStruct((fields, nx, modes), narrow),
            jax.ShapeDtypeStruct((fields, ny, modes), narrow),
            jax.ShapeDtypeStruct((fields, ny, modes), narrow),
        ),
        in_specs=[hbm] * 5,
        out_specs=(vmem,) * 5,
        scratch_shapes=[
            pltpu.VMEM((fields, nx, strip, modes), narrow),
            pltpu.VMEM((fields, nx, strip, modes), narrow),
            pltpu.VMEM((3, nx, ny), jnp.float32),
            pltpu.VMEM(eig_rows.shape, narrow),
            pltpu.SemaphoreType.DMA((8,)),
        ],
        compiler_params=pltpu.CompilerParams(vmem_limit_bytes=8 << 20),
        name="outline",
    )(*in_hbm)


def contract(left, right):
    return lax.dot_general(left, right, (((0,), (0,)), ((), ())), preferred_element_type=jnp.float32)


def finish_kernel(
    scale, gathered, order, g_ref, raw, ct_ref, head_x, tail_x, from_west, from_east, tail_y, from_north, vt_ref, out_ref, placed, image
):
    modes = g_ref.shape[0]
    ny = head_x.shape[1]
    nx = tail_y.shape[1]
    total = g_ref[...]

    def side(own, other, column, along, sign):
        half_c, half_rho, half_inverse, half_sound = (sign * c for c in column)
        spread_c = viscosity + half_c
        images = [
            half_c * other(0) + half_rho * other(along),
            spread_c * other(1),
            spread_c * other(2),
            spread_c * other(3),
            half_c * other(4) + half_sound * other(along),
        ]
        images[along] = images[along] + half_inverse * other(4)
        size = own.shape[1]
        for f in range(5):
            image[f * size : (f + 1) * size] = images[f].astype(jnp.bfloat16)
        return contract(own[0:5].reshape(5 * size, modes), image[0 : 5 * size])

    def plane(ref):
        return lambda f: ref[f].astype(jnp.float32)

    def column_x(i):
        return tuple(ct_ref[0:ny, j * nx + i : j * nx + i + 1] for j in (0, 2, 4, 5))

    total += side(head_x, plane(from_west), column_x(0), 1, -1.0)
    total += side(tail_x, plane(from_east), column_x(nx - 1), 1, 1.0)
    own_column = tuple(raw[j * nx : (j + 1) * nx, ny - 1 : ny] for j in (1, 2, 4, 5))
    packed = from_north[5].astype(jnp.float32)
    other_column = tuple(
        packed[:, 3 * j : 3 * j + 1] + packed[:, 3 * j + 1 : 3 * j + 2] + packed[:, 3 * j + 2 : 3 * j + 3]
        for j in range(4)
    )
    total += side(tail_y, plane(from_north), own_column, 2, 1.0)
    total += side(from_north, plane(tail_y), other_column, 2, -1.0)

    rows = modes // len(order)
    for place, tile in enumerate(gathered):
        placed[tile * rows : (tile + 1) * rows] = vt_ref[place].astype(jnp.float32)
    vt = placed[...].astype(jnp.bfloat16)
    right = None
    for part in split(total)[:2]:
        one = lax.dot_general(part, vt, (((1,), (1,)), ((), ())), preferred_element_type=jnp.float32)
        right = one if right is None else right + one
    both = None
    for part in split(right)[:2]:
        one = jnp.dot(vt, part, preferred_element_type=jnp.float32)
        both = one if both is None else both + one
    for place, tile in enumerate(order):
        out_ref[place] = (both[tile * rows : (tile + 1) * rows] * scale).astype(jnp.bfloat16)


def finish(scale, gathered, order, *operands):
    modes = operands[-1].shape[-1]
    return pl.pallas_call(
        functools.partial(finish_kernel, scale, gathered, order),
        out_shape=jax.ShapeDtypeStruct((len(order), modes // len(order), modes), jnp.bfloat16),
        in_specs=[pl.BlockSpec(memory_space=pltpu.VMEM)] * len(operands),
        out_specs=pl.BlockSpec(memory_space=pltpu.VMEM),
        scratch_shapes=[
            pltpu.VMEM((modes, modes), jnp.float32),
            pltpu.VMEM((480, modes), jnp.bfloat16),
        ],
        compiler_params=pltpu.CompilerParams(vmem_limit_bytes=12 << 20),
        name="finish",
    )(*operands)


def body(snapshots, eig_columns, mean_u, mean_v, mean_rho, mean_shear, sound):
    sections = lax.axis_size("sec")
    tiles_n = lax.axis_size("tile")
    fields, nx, ny, modes = snapshots.shape
    rows = modes // tiles_n
    scale = float(fields * nx * ny * sections * tiles_n) ** (-0.5)

    far = 4
    near = tiles_n // far
    wide = near // 2
    gathered = [
        ((x + 2) % wide * far + (z + 3) % far) * 2 + core
        for x in range(wide)
        for z in range(far)
        for core in range(2)
    ]
    summed = [
        ((x + wide // 2) % wide * far + (z + far // 2) % far) * 2 + core
        for x in range(wide)
        for z in range(far)
        for core in range(2)
    ]
    arrived = [(s + sections - 2) % sections for s in range(sections)]
    own, head_y, tail_y, head_x, tail_x = outline(
        snapshots, eig_columns.T, tiles_n, mean_v, mean_rho, sound
    )
    vt = lax.all_to_all(own, "tile", 0, 0, tiled=True, axis_index_groups=[gathered])
    from_north = lax.ppermute(head_y, "tile", [(i + 1, i) for i in range(tiles_n - 1)])
    from_west = lax.ppermute(tail_x, "sec", [(i, i + 1) for i in range(sections - 1)])
    from_east = lax.ppermute(head_x, "sec", [(i + 1, i) for i in range(sections - 1)])

    gram, raw, columns = interior(snapshots, mean_u, mean_v, mean_rho, mean_shear, sound)
    local = finish(
        scale, gathered, summed, gram, raw, columns, head_x, tail_x, from_west, from_east, tail_y, from_north, vt
    )
    shares = lax.all_to_all(local, "tile", 0, 0, tiled=True, axis_index_groups=[summed])
    term = shares.astype(jnp.float32).sum(0)
    terms = lax.all_to_all(
        jnp.broadcast_to(term[None], (sections, rows, modes)), "sec", 0, 0, tiled=True, axis_index_groups=[arrived]
    )
    upstream = jnp.array(arrived) <= lax.axis_index("sec")
    return jnp.where(upstream[:, None, None], terms, 0.0).sum(0)[None]


def solution(mesh):
    in_specs = (
        P(None, "sec", "tile", None),
        P(None, "tile"),
        P("sec", "tile"),
        P("sec", "tile"),
        P("sec", "tile"),
        P("sec", "tile"),
        P("sec", "tile"),
    )
    out_specs = P("sec", "tile", None)
    return jax.shard_map(body, mesh=mesh, in_specs=in_specs, out_specs=out_specs, check_vma=False)
```
